512 devices in a mesh: tensor: 8 (over x, core), context: 64 (over y, z).
Axes of the slice: x: 4, y: 4, z: 16, core: 2. Of those that a mesh axis runs over, the one named last changes fastest.
Arguments:
- q_proj: bfloat16 [16384, 8192], P('context', 'tensor'), may hold values from -6 to 6
- k_proj: bfloat16 [16384, 8192], P('context', 'tensor'), may hold values from -6 to 6
- v_proj: bfloat16 [16384, 8192], P('context', 'tensor'), may hold values from -6 to 6
- short_filter: bfloat16 [3, 3, 512], P(None, None, 'tensor'), may hold values from -3.5 to 3.5
- residue: float32 [16, 8192], P(None, 'tensor'), may hold values from -1.5 to 1.5
- decay_rate: float32 [16, 8192], P(None, 'tensor'), may hold values from 0.5 to 512
- out_weight: bfloat16 [4096, 8192], P('context', 'tensor'), may hold values from -0.0625 to 0.0625
Outputs:
- projected: bfloat16 [4096, 16384], P('tensor', 'context')
The draws below stay inside these ranges and needn't reach their ends.
All inputs are finite; a program needn't handle non-finite values.
Results may differ from the reference program's by a relative error of at most 0.02.
Values may be sent and summed in bfloat16 or wider, within the bound.
A program may use at most 128 MiB of HBM per device.

```python
import math
import jax
import jax.numpy as jnp
from jax import lax

D = 8192
DOUT = 4096
GROUP = 16
STAPS = 3
MODES = 16
TOKENS = 16384
GROUPS = 512
N_TENSOR = 8


def levels(rng, shape, shards, smallest, top_value):
    level = 1.0
    for dim, shards_of in shards:
        draws = jax.random.uniform(jax.random.fold_in(jax.random.fold_in(rng, 6), dim), (shards_of,), jnp.float32, smallest / len(shards), top_value / len(shards))
        level = level * jnp.repeat(jnp.exp(draws), shape[dim] // shards_of).reshape((-1,) + (1,) * (len(shape) - 1 - dim))
    return level


def normal_values(own_key, dims, deviation, limit, split=(), kind=jnp.bfloat16):
    drawn = deviation * jax.random.normal(own_key, dims, jnp.float32)
    if split:
        drawn = drawn * levels(own_key, dims, split, -0.22, 0.18)
    return jnp.clip(drawn, -limit, limit).astype(kind)


def setup_inputs(seed: int = 0) -> dict:
    arg_keys = jax.random.split(jax.random.key(seed), 8)
    q_proj = normal_values(arg_keys[0], (TOKENS, D), 1.0, 6.0, ((0, 64), (1, 8)))
    k_proj = normal_values(arg_keys[1], (TOKENS, D), 1.0, 6.0, ((0, 64), (1, 8)))
    v_proj = normal_values(arg_keys[2], (TOKENS, D), 1.0, 6.0, ((0, 64), (1, 8)))
    short_filter = normal_values(arg_keys[3], (3, STAPS, GROUPS), STAPS ** -0.5, 3.5, ((2, 8),))
    residue = normal_values(arg_keys[4], (MODES, D), 0.25, 1.5, ((1, 8),), jnp.float32)
    decay_rate = jnp.clip(jnp.exp(math.log(512.0) - 6.931472 * jax.random.uniform(arg_keys[5], (MODES, D), jnp.float32) ** levels(arg_keys[5], (MODES, D), ((1, 8),), -0.2, 0.2)), 0.5, 512.0)
    out_weight = normal_values(arg_keys[6], (DOUT, D), D ** -0.5, 0.0625, ((0, 64), (1, 8)))
    return dict(q_proj=q_proj, k_proj=k_proj, v_proj=v_proj, short_filter=short_filter, residue=residue, decay_rate=decay_rate, out_weight=out_weight)


def causal_taps(signal, filters):
    tap_count = filters.shape[0]
    length_rows = signal.shape[0]
    padded = jnp.pad(signal, ((tap_count - 1, 0), (0, 0)))
    running = jnp.zeros_like(signal)
    for offset in range(tap_count):
        begin = tap_count - 1 - offset
        running = running + filters[offset] * padded[begin:begin + length_rows]
    return running

def reference(q_proj, k_proj, v_proj, short_filter, residue, decay_rate, out_weight):
    chan_count = q_proj.shape[1]
    chan_block = math.gcd(chan_count, 256)
    block_total = chan_count // chan_block
    short_wide = jnp.repeat(short_filter.astype(jnp.float32), GROUP, axis=2)
    decay_step = decay_rate / TOKENS
    mode_scale = residue * jnp.sqrt(2.0 * decay_step)
    positions = jnp.arange(TOKENS).astype(jnp.float32)
    fft_length = 2 * TOKENS

    def one_block(block_index):
        first_chan = (block_index * chan_block).astype(jnp.int32)

        def columns(source, along_dim):
            return lax.dynamic_slice_in_dim(source, first_chan, chan_block, along_dim)
        q_feat = causal_taps(columns(q_proj, 1).astype(jnp.float32), columns(short_wide[0], 1)).astype(jnp.bfloat16)
        k_feat = causal_taps(columns(k_proj, 1).astype(jnp.float32), columns(short_wide[1], 1)).astype(jnp.bfloat16)
        v_feat = causal_taps(columns(v_proj, 1).astype(jnp.float32), columns(short_wide[2], 1)).astype(jnp.bfloat16)
        product = (k_feat.astype(jnp.float32) * v_feat.astype(jnp.float32)).astype(jnp.bfloat16)
        steps_block = columns(decay_step, 1)
        scale_block = columns(mode_scale, 1)
        response = jnp.zeros((TOKENS, chan_block), jnp.float32)
        for mode_index in range(MODES):
            response = response + scale_block[mode_index] * jnp.exp(-steps_block[mode_index] * positions[:, None])
        spectrum = jnp.fft.rfft(product.astype(jnp.float32), n=fft_length, axis=0) * jnp.fft.rfft(response, n=fft_length, axis=0)
        mixed = jnp.fft.irfft(spectrum, n=fft_length, axis=0)[:TOKENS].astype(jnp.float32)
        return (q_feat.astype(jnp.float32) * mixed).astype(jnp.bfloat16)
    stacked = lax.map(one_block, jnp.arange(block_total).astype(jnp.int32))
    gated = jnp.transpose(stacked, (1, 0, 2)).reshape(TOKENS, chan_count)
    shard_chans = chan_count // N_TENSOR
    running = jnp.zeros((DOUT, TOKENS), jnp.float32)
    for shard_index in range(N_TENSOR):
        low_chan = shard_index * shard_chans
        partial_term = lax.dot_general(out_weight[:, low_chan:low_chan + shard_chans], gated[:, low_chan:low_chan + shard_chans], (((1,), (1,)), ((), ())), preferred_element_type=jnp.float32)
        rounded = lax.optimization_barrier(partial_term.astype(jnp.bfloat16))
        running = running + rounded.astype(jnp.float32)
    return running.astype(jnp.bfloat16)
```

```python
import functools

import jax
import jax.numpy as jnp
from jax import lax
from jax.experimental import pallas as pl
from jax.experimental.pallas import tpu as pltpu
from jax.sharding import PartitionSpec as P

SPLIT = 4
RING = 16
LANES = 128
SUBL = 8


def front_kernel(q_ref, k_ref, v_ref, rim_ref, filt_ref, decay_ref, q3_ref, p3_ref, end_ref, ext):
    rows = q_ref.shape[0]

    def feature(which, src, lanes):
        ext[0:SUBL, :] = rim_ref[which, :, lanes]
        ext[SUBL : SUBL + rows, :] = src[:, lanes].astype(jnp.float32)
        total = filt_ref[3 * which : 3 * which + 1, lanes] * ext[SUBL : SUBL + rows, :]
        for tap in range(1, 3):
            total = total + filt_ref[3 * which + tap : 3 * which + tap + 1, lanes] * ext[
                SUBL - tap : SUBL - tap + rows, :
            ]
        return total.astype(jnp.bfloat16).astype(jnp.float32)

    for g in range(SUBL):
        lanes = slice(g * LANES, (g + 1) * LANES)
        spread = pl.ds(g, rows, stride=SUBL)
        k_feat = feature(1, k_ref, lanes)
        v_feat = feature(2, v_ref, lanes)
        p3_ref[spread, :] = (k_feat * v_feat).astype(jnp.bfloat16).astype(jnp.float32)
        q3_ref[spread, :] = feature(0, q_ref, lanes)

    modes = decay_ref.shape[0]
    decay = [decay_ref[m] for m in range(modes)]

    def step(lap, state):
        for u in range(8):
            p = p3_ref[pl.ds(pl.multiple_of((lap * 8 + u) * SUBL, SUBL), SUBL), :]
            state = tuple(a * s + p for a, s in zip(decay, state))
        return state

    zero = jnp.zeros((SUBL, LANES), jnp.float32)
    state = lax.fori_loop(0, rows // 8, step, (zero,) * modes)
    for m in range(modes):
        end_ref[m] = state[m]


def back_kernel(q3_ref, p3_ref, start_ref, decay_ref, scale_ref, gated_ref, g3):
    rows = gated_ref.shape[0]
    modes = decay_ref.shape[0]
    decay = [decay_ref[m] for m in range(modes)]
    scale = [scale_ref[m] for m in range(modes)]

    def step(lap, state):
        for u in range(4):
            here = pl.ds(pl.multiple_of((lap * 4 + u) * SUBL, SUBL), SUBL)
            p = p3_ref[here, :]
            state = tuple(a * s + p for a, s in zip(decay, state))
            terms = [c * s for c, s in zip(scale, state)]
            while len(terms) > 1:
                terms = [terms[i] + terms[i + 1] for i in range(0, len(terms), 2)]
            g3[here, :] = q3_ref[here, :] * terms[0]
        return state

    lax.fori_loop(0, rows // 4, step, tuple(start_ref[m] for m in range(modes)))
    for g in range(SUBL):
        gated_ref[:, g * LANES : (g + 1) * LANES] = g3[pl.ds(g, rows, stride=SUBL), :].astype(
            jnp.bfloat16
        )


def vmem_call(kernel, outs, scratch, flops, moved):
    return pl.pallas_call(
        kernel,
        out_shape=outs,
        scratch_shapes=scratch,
        cost_estimate=pl.CostEstimate(flops=flops, bytes_accessed=moved, transcendentals=0),
        compiler_params=pltpu.CompilerParams(vmem_limit_bytes=32 * 1024 * 1024),
    )


def context_shift(block, distance):
    count = lax.axis_size("context")
    return lax.ppermute(
        block, "context", [(i, i + distance) for i in range(count) if i + distance < count]
    )


def y_shift(block, distance):
    count = lax.axis_size("context")
    return lax.ppermute(
        block, "context", [(i, (i + distance * RING) % count) for i in range(count)]
    )


def z_shift(block, distance):
    count = lax.axis_size("context")
    return lax.ppermute(
        block,
        "context",
        [(i, i // RING * RING + (i + distance) % RING) for i in range(count)],
    )


def core_swap(block):
    count = lax.axis_size("tensor")
    return lax.ppermute(block, "tensor", [(i, i ^ 1) for i in range(count)])


def x_shift(block, distance):
    count = lax.axis_size("tensor")
    return lax.ppermute(block, "tensor", [(i, (i + 2 * distance) % count) for i in range(count)])


def pick(block, index, axis=0):
    return lax.dynamic_index_in_dim(block, index, axis, keepdims=False)


def gather_weight(out_weight, y, z):
    rows, chans = out_weight.shape
    sub = rows // SPLIT
    pieces = out_weight.reshape(SPLIT, sub, chans)
    column = jnp.zeros_like(pieces)
    for dy in range(SPLIT):
        piece = pick(pieces, (y + dy) % SPLIT)
        if dy:
            piece = y_shift(piece, dy)
        column = lax.dynamic_update_index_in_dim(column, piece, (y - dy) % SPLIT, 0)
    parts = [(column, 0)]
    ahead = behind = column
    for lap in range(1, RING // 2 + 1):
        ahead = z_shift(ahead, 1)
        parts.append((ahead, -lap))
        if lap < RING // 2:
            behind = z_shift(behind, -1)
            parts.append((behind, lap))
    whole = jnp.zeros((SPLIT, RING, sub, chans), out_weight.dtype)
    for part, offset in parts:
        whole = lax.dynamic_update_index_in_dim(whole, part, (z + offset) % RING, 1)
    return whole.reshape(SPLIT * RING * sub, chans)


def add_over_tensor(partial, x, core):
    blocks = partial.reshape(SPLIT, 2, -1, partial.shape[-1])
    kept = pick(blocks, core, 1).astype(jnp.float32)
    came = core_swap(pick(blocks, 1 - core, 1)).astype(jnp.float32)
    paired = (kept + came).astype(jnp.bfloat16)
    total = pick(paired, x).astype(jnp.float32)
    for dx in range(1, SPLIT):
        total = total + x_shift(pick(paired, (x + dx) % SPLIT), dx).astype(jnp.float32)
    return total.astype(jnp.bfloat16)


def per_device(q_proj, k_proj, v_proj, short_filter, residue, decay_rate, out_weight):
    row_count, chan_count = q_proj.shape
    modes = residue.shape[0]
    taps = short_filter.shape[1]
    group_width = chan_count // short_filter.shape[2]
    place = lax.axis_index("context")
    y, z = place // RING, place % RING
    seat = lax.axis_index("tensor")
    x, core = seat // 2, seat % 2

    rim = jnp.stack([a[row_count - (taps - 1) :] for a in (q_proj, k_proj, v_proj)])
    rim = context_shift(rim, 1).astype(jnp.float32)
    rim = jnp.pad(rim, ((0, 0), (SUBL - (taps - 1), 0), (0, 0)))
    filters = jnp.repeat(
        short_filter.astype(jnp.float32).reshape(3 * taps, -1), group_width, axis=1
    )
    decay_step = (decay_rate / (row_count * lax.axis_size("context"))).reshape(modes, SUBL, LANES)
    mode_scale = residue.reshape(modes, SUBL, LANES) * jnp.sqrt(2.0 * decay_step)
    decay = jnp.exp(-decay_step)

    def block_decay(blocks):
        return jnp.exp(-decay_step * (row_count * blocks))

    wide = jax.ShapeDtypeStruct((row_count * SUBL, LANES), jnp.float32)
    state = jax.ShapeDtypeStruct((modes, SUBL, LANES), jnp.float32)
    elements = row_count * chan_count
    q3, p3, ends = vmem_call(
        front_kernel,
        (wide, wide, state),
        [pltpu.VMEM((row_count + SUBL, LANES), jnp.float32)],
        elements * 60,
        elements * 14,
    )(q_proj, k_proj, v_proj, rim, filters, decay)

    sent = ends.astype(jnp.bfloat16)
    start = context_shift(sent, 1).astype(jnp.float32)
    for d in range(2, 5):
        start = start + block_decay(d - 1) * context_shift(sent, d).astype(jnp.float32)
    for unit in (4, 16):
        sent = start.astype(jnp.bfloat16)
        for d in range(1, 4):
            start = start + block_decay(d * unit) * context_shift(sent, d * unit).astype(
                jnp.float32
            )

    gated = vmem_call(
        back_kernel,
        jax.ShapeDtypeStruct((row_count, chan_count), jnp.bfloat16),
        [pltpu.VMEM((row_count * SUBL, LANES), jnp.float32)],
        elements * 66,
        elements * 10,
    )(q3, p3, start, decay, mode_scale)

    weight = gather_weight(out_weight, y, z)
    share = out_weight.shape[0] // SPLIT
    result = jnp.zeros((share // 2, SPLIT, share, row_count), jnp.bfloat16)
    for dy in (0, 1, 3, 2):
        tokens = y_shift(gated, dy) if dy else gated
        partial = lax.dot_general(
            weight, tokens, (((1,), (1,)), ((), ())), preferred_element_type=jnp.float32
        ).astype(jnp.bfloat16)
        summed = add_over_tensor(partial, x, core)
        if dy:
            summed = y_shift(summed, -dy)
        result = lax.dynamic_update_index_in_dim(
            result, summed.reshape(share // 2, share, row_count), (y + dy) % SPLIT, 1
        )
    return result.reshape(share // 2 * SPLIT * share, row_count)


def solution(mesh):
    return jax.shard_map(
        per_device,
        mesh=mesh,
        in_specs=(
            P("context", "tensor"),
            P("context", "tensor"),
            P("context", "tensor"),
            P(None, None, "tensor"),
            P(None, "tensor"),
            P(None, "tensor"),
            P("context", "tensor"),
        ),
        out_specs=P("tensor", "context"),
        check_vma=False,
    )
```

```python
import functools

import jax
import jax.numpy as jnp
from jax import lax
from jax.experimental import pallas as pl
from jax.experimental.pallas import tpu as pltpu
from jax.sharding import PartitionSpec as P

SPLIT = 4
RING = 16
LANES = 128
SUBL = 8
UP, DOWN = 6, 9
FAR = (1, 2, 3, 4, 8, 12)
COPIES = 128


def mixer_kernel(
    total_rows, q_ref, k_ref, v_ref, filt_ref, residue_ref, rate_ref, w_ref, out_ref,
    ext, head, p3, q3, g3, wide, rim_out, rim_in, st_out, st_in, whole, tokens,
    part, swapped, paired, crossed, summed, homed, send_sem, recv_sem,
):
    rows = q_ref.shape[0]
    modes = rate_ref.shape[0]
    sub = w_ref.shape[1]
    place = lax.axis_index("context")
    blocks = lax.axis_size("context")
    y, z = place // RING, place % RING
    seat = lax.axis_index("tensor")
    x, core = seat // 2, seat % 2

    def on_context(distance):
        return {"context": lax.rem(place + (distance + blocks), blocks)}

    def on_ring(distance):
        return {"context": y * RING + lax.rem(z + (distance + RING), RING)}

    def on_x(distance):
        return {"tensor": lax.rem(seat + 2 * distance, 2 * SPLIT)}

    other_core = {"tensor": x * 2 + (1 - core)}
    peers = [on_context(d) for d in FAR] + [on_context(-d) for d in FAR]
    peers += [on_context(d * RING) for d in range(1, SPLIT)]
    peers += [on_ring(1), on_ring(-1), other_core]
    peers += [on_x(d) for d in range(1, SPLIT)]
    barrier = pltpu.get_barrier_semaphore()
    for peer in peers:
        pl.semaphore_signal(barrier, inc=1, device_id=peer, device_id_type=pl.DeviceIdType.MESH)

    started = []

    def send(src, dst, peer):
        index = len(started)
        copy = pltpu.make_async_remote_copy(
            src_ref=src,
            dst_ref=dst,
            send_sem=send_sem.at[index],
            recv_sem=recv_sem.at[index],
            device_id=peer,
            device_id_type=pl.DeviceIdType.MESH,
        )
        copy.start()
        started.append(copy)
        return copy

    rim_out[...] = jnp.zeros_like(rim_out)
    for n, src in enumerate((q_ref, k_ref, v_ref)):
        rim_out[2 * n : 2 * n + 2, :] = src[rows - 16 : rows, :].astype(jnp.float32)[14:16]

    def feature(which, src, lanes):
        ext[0:SUBL, :] = jnp.zeros((SUBL, LANES), jnp.float32)
        ext[SUBL : SUBL + rows, :] = src[:, lanes].astype(jnp.float32)
        total = filt_ref[3 * which : 3 * which + 1, lanes] * ext[SUBL : SUBL + rows, :]
        for tap in range(1, 3):
            total = total + filt_ref[3 * which + tap : 3 * which + tap + 1, lanes] * ext[
                SUBL - tap : SUBL - tap + rows, :
            ]
        return total.astype(jnp.bfloat16).astype(jnp.float32)

    for g in range(SUBL):
        lanes = slice(g * LANES, (g + 1) * LANES)
        spread = pl.ds(g, rows, stride=SUBL)
        k_feat = feature(1, k_ref, lanes)
        v_feat = feature(2, v_ref, lanes)
        p3[spread, :] = (k_feat * v_feat).astype(jnp.bfloat16).astype(jnp.float32)
        q3[spread, :] = feature(0, q_ref, lanes)
        wide[0, pl.ds(g, modes, stride=SUBL), :] = rate_ref[:, lanes] / total_rows
        wide[1, pl.ds(g, modes, stride=SUBL), :] = residue_ref[:, lanes]
    decay_step = wide[0]
    wide[2] = jnp.exp(-decay_step)
    wide[1] = wide[1] * jnp.sqrt(2.0 * decay_step)

    def mode_rows(slot):
        return [wide[slot, m * SUBL : (m + 1) * SUBL, :] for m in range(modes)]

    def run(first, last, state, gate):
        decay = mode_rows(2)
        scale = mode_rows(1) if gate else None
        unroll = 4

        def step(lap, state):
            for u in range(unroll):
                at = pl.ds(pl.multiple_of((lap * unroll + u) * SUBL, SUBL), SUBL)
                p = p3[at, :]
                state = tuple(a * s + p for a, s in zip(decay, state))
                if gate:
                    terms = [c * s for c, s in zip(scale, state)]
                    while len(terms) > 1:
                        terms = [terms[i] + terms[i + 1] for i in range(0, len(terms), 2)]
                    g3[at, :] = q3[at, :] * terms[0]
            return state

        return lax.fori_loop(first // unroll, last // unroll, step, state)

    zero = jnp.zeros((SUBL, LANES), jnp.float32)
    body_end = run(SUBL, rows, (zero,) * modes, False)
    whole[z, y] = w_ref[y]

    pl.semaphore_wait(barrier, len(peers))
    rim_copy = send(rim_out, rim_in, on_context(1))
    column = [None] + [
        send(w_ref.at[lax.rem(y + dy, SPLIT)], whole.at[z, y], on_context(dy * RING))
        for dy in range(1, SPLIT)
    ]

    def from_y(dy):
        return lax.rem(y + (SPLIT - dy), SPLIT)

    up = [[None] * SPLIT for _ in range(UP + 1)]
    down = [[None] * SPLIT for _ in range(DOWN + 1)]

    def ring(lap):
        for dy in range(SPLIT):
            source = from_y(dy)
            if lap == 0:
                if dy:
                    column[dy].wait_recv()
            for laps, count, sign in ((up, UP, 1), (down, DOWN, -1)):
                if lap > count:
                    continue
                if lap:
                    laps[lap][dy].wait_recv()
                if lap < count:
                    slot = whole.at[lax.rem(z + (RING - sign * lap), RING), source]
                    block = w_ref.at[y] if lap == 0 and dy == 0 else slot
                    laps[lap + 1][dy] = send(block, slot, on_ring(sign))

    rim_copy.wait_recv()
    rim = jnp.where(place > 0, rim_in[...], 0.0)
    feats = []
    for n, src in enumerate((q_ref, k_ref, v_ref)):
        head[0:SUBL, :] = jnp.zeros((SUBL, head.shape[1]), jnp.float32)
        head[SUBL - 2 : SUBL, :] = rim[2 * n : 2 * n + 2]
        head[SUBL : 2 * SUBL, :] = src[0:16, :].astype(jnp.float32)[0:SUBL]
        total = filt_ref[3 * n : 3 * n + 1, :] * head[SUBL : 2 * SUBL, :]
        for tap in range(1, 3):
            total = total + filt_ref[3 * n + tap : 3 * n + tap + 1, :] * head[
                SUBL - tap : 2 * SUBL - tap, :
            ]
        feats.append(total.astype(jnp.bfloat16).astype(jnp.float32))
    first_product = (feats[1] * feats[2]).astype(jnp.bfloat16).astype(jnp.float32)
    for g in range(SUBL):
        lanes = slice(g * LANES, (g + 1) * LANES)
        p3[pl.ds(g, SUBL, stride=SUBL), :] = first_product[:, lanes]
        q3[pl.ds(g, SUBL, stride=SUBL), :] = feats[0][:, lanes]
    head_end = jnp.concatenate(run(0, SUBL, (zero,) * modes, False), axis=0)
    state = jnp.concatenate(body_end, axis=0) + jnp.exp(-decay_step * (rows - SUBL)) * head_end

    def start_round(slot, first_copy, distances):
        return [
            send(st_out.at[slot], st_in.at[first_copy + i], on_context(d))
            for i, d in enumerate(distances)
        ]

    def end_round(copies, first_copy, distances, lead, total):
        for i, d in enumerate(distances):
            copies[i].wait_recv()
            came = jnp.where(place >= d, st_in[first_copy + i].astype(jnp.float32), 0.0)
            if d != lead:
                came = came * jnp.exp(-decay_step * (rows * (d - lead)))
            total = came if total is None else total + came
        return total

    st_out[0] = state.astype(jnp.bfloat16)
    near = (1, 2, 3, 4)
    copies = start_round(0, 0, near)
    ring(0)
    ring(1)
    state = end_round(copies, 0, near, 1, None)
    st_out[1] = state.astype(jnp.bfloat16)
    middle = (4, 8, 12)
    copies = start_round(1, 4, middle)
    ring(2)
    ring(3)
    ring(4)
    state = end_round(copies, 4, middle, 0, state)
    st_out[2] = state.astype(jnp.bfloat16)
    distant = (16, 32, 48)
    copies = start_round(2, 7, distant)
    ring(5)
    state = end_round(copies, 7, distant, 0, state)

    run(0, rows, tuple(state[m * SUBL : (m + 1) * SUBL] for m in range(modes)), True)
    for g in range(SUBL):
        gated = g3[pl.ds(g, rows, stride=SUBL), :].astype(jnp.bfloat16)
        tokens[0, 0, :, g * LANES : (g + 1) * LANES] = gated[: rows // 2]
        tokens[0, 1, :, g * LANES : (g + 1) * LANES] = gated[rows // 2 :]

    from_below, from_above = on_context(RING), on_context(-RING)
    low = [send(tokens.at[0, h], tokens.at[1, h], from_below) for h in (0, 1)]
    high = [send(tokens.at[0, h], tokens.at[3, h], from_above) for h in (1, 0)]
    ring(6)
    ring(7)
    low[0].wait_recv()
    across = [send(tokens.at[1, 0], tokens.at[2, 0], from_below)]
    high[0].wait_recv()
    across.append(send(tokens.at[3, 1], tokens.at[2, 1], from_above))
    ring(8)
    ring(9)

    share = SUBL * sub

    def multiply(dy):
        rhs = tokens[dy].reshape(rows, -1)
        for half in range(2):
            lhs = whole[half * SUBL : (half + 1) * SUBL].reshape(SPLIT * share, -1)
            terms = lax.dot_general(
                lhs, rhs, (((1,), (1,)), ((), ())), preferred_element_type=jnp.float32
            ).astype(jnp.bfloat16)
            terms = terms.reshape(SUBL, SPLIT, sub, rows)
            for col in range(SPLIT):
                part[dy, half, col] = terms[:, col].reshape(share, rows)
        return send(part.at[dy, 1 - core], swapped.at[dy], other_core)

    def pair(dy, copy):
        copy.wait_recv()
        both = part[dy, core].astype(jnp.float32) + swapped[dy].astype(jnp.float32)
        paired[dy] = both.astype(jnp.bfloat16)
        return [
            send(paired.at[dy, lax.rem(x + dx, SPLIT)], crossed.at[dy, dx - 1], on_x(dx))
            for dx in range(1, SPLIT)
        ]

    def finish(dy, copies):
        total = paired[dy, x].astype(jnp.float32)
        for dx in range(1, SPLIT):
            copies[dx - 1].wait_recv()
            total = total + crossed[dy, dx - 1].astype(jnp.float32)
        total = total.astype(jnp.bfloat16)
        if dy == 0:
            out_ref[:, y] = total.reshape(SUBL, sub, rows)
            return None
        summed[dy - 1] = total
        return send(summed.at[dy - 1], homed.at[dy - 1], on_context(-dy * RING))

    swap0 = multiply(0)
    low[1].wait_recv()
    swap1 = multiply(1)
    cross0 = pair(0, swap0)
    high[1].wait_recv()
    swap3 = multiply(3)
    cross1 = pair(1, swap1)
    finish(0, cross0)
    for copy in across:
        copy.wait_recv()
    swap2 = multiply(2)
    cross3 = pair(3, swap3)
    home1 = finish(1, cross1)
    cross2 = pair(2, swap2)
    home3 = finish(3, cross3)
    home2 = finish(2, cross2)
    for dy, copy in ((1, home1), (3, home3), (2, home2)):
        copy.wait_recv()
        out_ref[:, lax.rem(y + dy, SPLIT)] = homed[dy - 1].reshape(SUBL, sub, rows)
    for copy in started:
        copy.wait_send()


def per_device(q_proj, k_proj, v_proj, short_filter, residue, decay_rate, out_weight):
    rows, chans = q_proj.shape
    modes = residue.shape[0]
    taps = short_filter.shape[1]
    group_width = chans // short_filter.shape[2]
    sub = out_weight.shape[0] // SPLIT
    share = SUBL * sub
    filters = jnp.repeat(
        short_filter.astype(jnp.float32).reshape(3 * taps, -1), group_width, axis=1
    )
    f32, bf16 = jnp.float32, jnp.bfloat16
    scratch = [
        ((rows + SUBL, LANES), f32),
        ((2 * SUBL, chans), f32),
        ((rows * SUBL, LANES), f32),
        ((rows * SUBL, LANES), f32),
        ((rows * SUBL, LANES), f32),
        ((3, modes * SUBL, LANES), f32),
        ((SUBL, chans), f32),
        ((SUBL, chans), f32),
        ((3, modes * SUBL, LANES), bf16),
        ((10, modes * SUBL, LANES), bf16),
        ((RING, SPLIT, sub, chans), bf16),
        ((SPLIT, 2, rows // 2, chans), bf16),
        ((SPLIT, 2, SPLIT, share, rows), bf16),
        ((SPLIT, SPLIT, share, rows), bf16),
        ((SPLIT, SPLIT, share, rows), bf16),
        ((SPLIT, SPLIT - 1, share, rows), bf16),
        ((SPLIT - 1, share, rows), bf16),
        ((SPLIT - 1, share, rows), bf16),
    ]
    result = pl.pallas_call(
        functools.partial(mixer_kernel, rows * lax.axis_size("context")),
        out_shape=jax.ShapeDtypeStruct((SUBL, SPLIT, sub, rows), bf16),
        in_specs=[pl.BlockSpec(memory_space=pltpu.VMEM)] * 7,
        out_specs=pl.BlockSpec(memory_space=pltpu.VMEM),
        scratch_shapes=[pltpu.VMEM(shape, kind) for shape, kind in scratch]
        + [pltpu.SemaphoreType.DMA((COPIES,))] * 2,
        compiler_params=pltpu.CompilerParams(
            collective_id=0, has_side_effects=True, vmem_limit_bytes=48 * 1024 * 1024
        ),
    )(
        q_proj, k_proj, v_proj, filters, residue, decay_rate,
        out_weight.reshape(SPLIT, sub, chans),
    )
    return result.reshape(SUBL * SPLIT * sub, rows)


def solution(mesh):
    return jax.shard_map(
        per_device,
        mesh=mesh,
        in_specs=(
            P("context", "tensor"),
            P("context", "tensor"),
            P("context", "tensor"),
            P(None, None, "tensor"),
            P(None, "tensor"),
            P(None, "tensor"),
            P("context", "tensor"),
        ),
        out_specs=P("tensor", "context"),
        check_vma=False,
    )
```

```python
import functools

import jax
import jax.numpy as jnp
from jax import lax
from jax.experimental import pallas as pl
from jax.experimental.pallas import tpu as pltpu
from jax.sharding import PartitionSpec as P

SPLIT = 4
RING = 16
LANES = 128
SUBL = 8
UP, DOWN = 7, 8
COPIES = 128


def mixer_kernel(
    total_rows, q_hbm, k_hbm, v_hbm, short_hbm, residue_hbm, rate_hbm, w_hbm, out_ref,
    q_ref, k_ref, v_ref, short_ref, residue_ref, rate_ref, w_ref, filt_ref, ext, head, p3, q3, g3, wide, rim_out, rim_in, st_out, st_in, whole, tokens,
    part, swapped, paired, crossed, summed, homed, send_sem, recv_sem, load_sem,
):
    rows = q_ref.shape[0]
    modes = rate_ref.shape[0]
    sub = w_ref.shape[1]
    place = lax.axis_index("context")
    blocks = lax.axis_size("context")
    y, z = place // RING, place % RING
    seat = lax.axis_index("tensor")
    x, core = seat // 2, seat % 2

    def on_context(distance):
        return {"context": lax.rem(place + (distance + blocks), blocks)}

    def on_ring(distance):
        return {"context": y * RING + lax.rem(z + (distance + RING), RING)}

    def on_x(distance):
        return {"tensor": lax.rem(seat + 2 * distance, 2 * SPLIT)}

    other_core = {"tensor": x * 2 + (1 - core)}
    peers = [on_context(1), on_context(-1)]
    peers += [on_context(d * RING) for d in range(1, SPLIT)]
    peers += [on_ring(1), on_ring(-1), other_core]
    peers += [on_x(d) for d in range(1, SPLIT)]
    barrier = pltpu.get_barrier_semaphore()
    for peer in peers:
        pl.semaphore_signal(barrier, inc=1, device_id=peer, device_id_type=pl.DeviceIdType.MESH)

    loads = []
    for src, dst in (
        (k_hbm, k_ref), (v_hbm, v_ref), (q_hbm, q_ref), (short_hbm, short_ref),
        (rate_hbm, rate_ref), (residue_hbm, residue_ref), (w_hbm, w_ref),
    ):
        loads.append(pltpu.make_async_copy(src, dst, load_sem.at[len(loads)]))
        loads[-1].start()

    started = []

    def send(src, dst, peer):
        index = len(started)
        copy = pltpu.make_async_remote_copy(
            src_ref=src,
            dst_ref=dst,
            send_sem=send_sem.at[index],
            recv_sem=recv_sem.at[index],
            device_id=peer,
            device_id_type=pl.DeviceIdType.MESH,
        )
        copy.start()
        started.append(copy)
        return copy

    taps, groups = short_ref.shape[1:]
    chans = q_ref.shape[1]
    owner = lax.broadcasted_iota(jnp.int32, (groups, chans), 1) // (chans // groups)
    own = owner == lax.broadcasted_iota(jnp.int32, (groups, chans), 0)
    spreader = jnp.where(own, 1.0, 0.0).astype(jnp.bfloat16)
    for load in loads:
        load.wait()
    for n in range(3):
        filt_ref[n, 0:taps, :] = lax.dot_general(
            short_ref[n], spreader, (((1,), (0,)), ((), ())), preferred_element_type=jnp.float32
        )
    rim_out[...] = jnp.zeros_like(rim_out)
    for n, src in enumerate((q_ref, k_ref, v_ref)):
        rim_out[2 * n : 2 * n + 2, :] = src[rows - 16 : rows, :].astype(jnp.float32)[14:16]

    def feature(which, src, lanes):
        ext[0:SUBL, :] = jnp.zeros((SUBL, LANES), jnp.float32)
        ext[SUBL : SUBL + rows, :] = src[:, lanes].astype(jnp.float32)
        total = filt_ref[which, 0:1, lanes] * ext[SUBL : SUBL + rows, :]
        for tap in range(1, 3):
            total = total + filt_ref[which, tap : tap + 1, lanes] * ext[
                SUBL - tap : SUBL - tap + rows, :
            ]
        return total.astype(jnp.bfloat16).astype(jnp.float32)

    for g in range(SUBL):
        lanes = slice(g * LANES, (g + 1) * LANES)
        spread = pl.ds(g, rows, stride=SUBL)
        k_feat = feature(1, k_ref, lanes)
        v_feat = feature(2, v_ref, lanes)
        p3[spread, :] = (k_feat * v_feat).astype(jnp.bfloat16).astype(jnp.float32)
        q3[spread, :] = feature(0, q_ref, lanes)
        wide[0, pl.ds(g, modes, stride=SUBL), :] = rate_ref[:, lanes] / total_rows
        wide[1, pl.ds(g, modes, stride=SUBL), :] = residue_ref[:, lanes]
    decay_step = wide[0]
    wide[2] = jnp.exp(-decay_step)
    wide[1] = wide[1] * jnp.sqrt(2.0 * decay_step)

    def mode_rows(slot):
        return [wide[slot, m * SUBL : (m + 1) * SUBL, :] for m in range(modes)]

    def run(first, last, state, gate):
        decay = mode_rows(2)
        scale = mode_rows(1) if gate else None
        unroll = 4

        def step(lap, state):
            for u in range(unroll):
                at = pl.ds(pl.multiple_of((lap * unroll + u) * SUBL, SUBL), SUBL)
                p = p3[at, :]
                state = tuple(a * s + p for a, s in zip(decay, state))
                if gate:
                    terms = [c * s for c, s in zip(scale, state)]
                    while len(terms) > 1:
                        terms = [terms[i] + terms[i + 1] for i in range(0, len(terms), 2)]
                    g3[at, :] = q3[at, :] * terms[0]
            return state

        return lax.fori_loop(first // unroll, last // unroll, step, state)

    zero = jnp.zeros((SUBL, LANES), jnp.float32)
    body_end = run(SUBL, rows, (zero,) * modes, False)
    whole[z, y] = w_ref[y]

    pl.semaphore_wait(barrier, len(peers))
    rim_copy = send(rim_out, rim_in, on_context(1))
    column = [None] + [
        send(w_ref.at[lax.rem(y + dy, SPLIT)], whole.at[z, y], on_context(dy * RING))
        for dy in range(1, SPLIT)
    ]

    def from_y(dy):
        return lax.rem(y + (SPLIT - dy), SPLIT)

    up = [[None] * SPLIT for _ in range(UP + 1)]
    down = [[None] * SPLIT for _ in range(DOWN + 1)]

    def ring(lap):
        for dy in range(SPLIT):
            source = from_y(dy)
            if lap == 0:
                if dy:
                    column[dy].wait_recv()
            for laps, count, sign in ((up, UP, 1), (down, DOWN, -1)):
                if lap > count:
                    continue
                if lap:
                    laps[lap][dy].wait_recv()
                if lap < count:
                    slot = whole.at[lax.rem(z + (RING - sign * lap), RING), source]
                    block = w_ref.at[y] if lap == 0 and dy == 0 else slot
                    laps[lap + 1][dy] = send(block, slot, on_ring(sign))

    rim_copy.wait_recv()
    rim = jnp.where(place > 0, rim_in[...], 0.0)
    feats = []
    for n, src in enumerate((q_ref, k_ref, v_ref)):
        head[0:SUBL, :] = jnp.zeros((SUBL, head.shape[1]), jnp.float32)
        head[SUBL - 2 : SUBL, :] = rim[2 * n : 2 * n + 2]
        head[SUBL : 2 * SUBL, :] = src[0:16, :].astype(jnp.float32)[0:SUBL]
        total = filt_ref[n, 0:1, :] * head[SUBL : 2 * SUBL, :]
        for tap in range(1, 3):
            total = total + filt_ref[n, tap : tap + 1, :] * head[
                SUBL - tap : 2 * SUBL - tap, :
            ]
        feats.append(total.astype(jnp.bfloat16).astype(jnp.float32))
    first_product = (feats[1] * feats[2]).astype(jnp.bfloat16).astype(jnp.float32)
    for g in range(SUBL):
        lanes = slice(g * LANES, (g + 1) * LANES)
        p3[pl.ds(g, SUBL, stride=SUBL), :] = first_product[:, lanes]
        q3[pl.ds(g, SUBL, stride=SUBL), :] = feats[0][:, lanes]
    head_end = jnp.concatenate(run(0, SUBL, (zero,) * modes, False), axis=0)
    state = jnp.concatenate(body_end, axis=0) + jnp.exp(-decay_step * (rows - SUBL)) * head_end

    half = RING // 2
    st_out[0] = state.astype(jnp.bfloat16)
    carried = {
        (1, 1): send(st_out.at[0], st_in.at[0], on_ring(1)),
        (-1, 1): send(st_out.at[0], st_in.at[half], on_ring(-1)),
    }
    before = jnp.zeros_like(state)
    after = state * jnp.exp(-decay_step * (rows * (RING - 1)))

    def turn(lap, before, after):
        for sign, count in ((1, half), (-1, half - 1)):
            if lap > count:
                continue
            slot = lap - 1 if sign > 0 else half + lap - 1
            carried[sign, lap].wait_recv()
            if lap < count:
                carried[sign, lap + 1] = send(st_in.at[slot], st_in.at[slot + 1], on_ring(sign))
        for sign, count in ((1, half), (-1, half - 1)):
            if lap > count:
                continue
            slot = lap - 1 if sign > 0 else half + lap - 1
            distance = lap if sign > 0 else RING - lap
            came = st_in[slot].astype(jnp.float32)
            if distance > 1:
                came = came * jnp.exp(-decay_step * (rows * (distance - 1)))
            earlier = z >= distance
            before = before + jnp.where(earlier, came, 0.0)
            after = after + jnp.where(earlier, 0.0, came)
        return before, after

    for lap in range(1, half + 1):
        before, after = turn(lap, before, after)
        if lap % 4:
            ring(lap - 1 - lap // 4)
    st_out[1] = (after + jnp.exp(-decay_step * (rows * RING)) * before).astype(jnp.bfloat16)
    rows_after = [
        send(st_out.at[1], st_in.at[RING - 2 + d], on_context(d * RING)) for d in range(1, SPLIT)
    ]
    ring(6)
    state = before
    for d in range(1, SPLIT):
        rows_after[d - 1].wait_recv()
        came = jnp.where(y >= d, st_in[RING - 2 + d].astype(jnp.float32), 0.0)
        if d > 1:
            came = came * jnp.exp(-decay_step * (rows * RING * (d - 1)))
        state = state + came

    run(0, rows, tuple(state[m * SUBL : (m + 1) * SUBL] for m in range(modes)), True)
    for g in range(SUBL):
        gated = g3[pl.ds(g, rows, stride=SUBL), :].astype(jnp.bfloat16)
        tokens[0, 0, :, g * LANES : (g + 1) * LANES] = gated[: rows // 2]
        tokens[0, 1, :, g * LANES : (g + 1) * LANES] = gated[rows // 2 :]

    from_below, from_above = on_context(RING), on_context(-RING)
    low = [send(tokens.at[0, h], tokens.at[1, h], from_below) for h in (0, 1)]
    high = [send(tokens.at[0, h], tokens.at[3, h], from_above) for h in (1, 0)]
    ring(7)
    low[0].wait_recv()
    across = [send(tokens.at[1, 0], tokens.at[2, 0], from_below)]
    high[0].wait_recv()
    across.append(send(tokens.at[3, 1], tokens.at[2, 1], from_above))
    ring(8)


    share = SUBL * sub

    def multiply(dy):
        rhs = tokens[dy].reshape(rows, -1)
        for half in range(2):
            lhs = whole[half * SUBL : (half + 1) * SUBL].reshape(SPLIT * share, -1)
            terms = lax.dot_general(
                lhs, rhs, (((1,), (1,)), ((), ())), preferred_element_type=jnp.float32
            ).astype(jnp.bfloat16)
            terms = terms.reshape(SUBL, SPLIT, sub, rows)
            for col in range(SPLIT):
                part[dy, half, col] = terms[:, col].reshape(share, rows)
        return send(part.at[dy, 1 - core], swapped.at[dy], other_core)

    def pair(dy, copy):
        copy.wait_recv()
        both = part[dy, core].astype(jnp.float32) + swapped[dy].astype(jnp.float32)
        paired[dy] = both.astype(jnp.bfloat16)
        return [
            send(paired.at[dy, lax.rem(x + dx, SPLIT)], crossed.at[dy, dx - 1], on_x(dx))
            for dx in range(1, SPLIT)
        ]

    def finish(dy, copies):
        total = paired[dy, x].astype(jnp.float32)
        for dx in range(1, SPLIT):
            copies[dx - 1].wait_recv()
            total = total + crossed[dy, dx - 1].astype(jnp.float32)
        total = total.astype(jnp.bfloat16)
        if dy == 0:
            out_ref[:, y] = total.reshape(SUBL, sub, rows)
            return None
        summed[dy - 1] = total
        return send(summed.at[dy - 1], homed.at[dy - 1], on_context(-dy * RING))

    swap0 = multiply(0)
    low[1].wait_recv()
    swap1 = multiply(1)
    cross0 = pair(0, swap0)
    high[1].wait_recv()
    swap3 = multiply(3)
    cross1 = pair(1, swap1)
    finish(0, cross0)
    for copy in across:
        copy.wait_recv()
    swap2 = multiply(2)
    cross3 = pair(3, swap3)
    home1 = finish(1, cross1)
    cross2 = pair(2, swap2)
    home3 = finish(3, cross3)
    home2 = finish(2, cross2)
    for dy, copy in ((1, home1), (3, home3), (2, home2)):
        copy.wait_recv()
        out_ref[:, lax.rem(y + dy, SPLIT)] = homed[dy - 1].reshape(SUBL, sub, rows)
    for copy in started:
        copy.wait_send()


def per_device(q_proj, k_proj, v_proj, short_filter, residue, decay_rate, out_weight):
    rows, chans = q_proj.shape
    modes = residue.shape[0]
    sub = out_weight.shape[0] // SPLIT
    share = SUBL * sub
    f32, bf16 = jnp.float32, jnp.bfloat16
    scratch = [
        ((rows, chans), bf16),
        ((rows, chans), bf16),
        ((rows, chans), bf16),
        (short_filter.shape, bf16),
        (residue.shape, f32),
        (decay_rate.shape, f32),
        ((SPLIT, sub, chans), bf16),
        ((3, SUBL, chans), f32),
        ((rows + SUBL, LANES), f32),
        ((2 * SUBL, chans), f32),
        ((rows * SUBL, LANES), f32),
        ((rows * SUBL, LANES), f32),
        ((rows * SUBL, LANES), f32),
        ((3, modes * SUBL, LANES), f32),
        ((SUBL, chans), f32),
        ((SUBL, chans), f32),
        ((2, modes * SUBL, LANES), bf16),
        ((RING + 2, modes * SUBL, LANES), bf16),
        ((RING, SPLIT, sub, chans), bf16),
        ((SPLIT, 2, rows // 2, chans), bf16),
        ((SPLIT, 2, SPLIT, share, rows), bf16),
        ((SPLIT, SPLIT, share, rows), bf16),
        ((SPLIT, SPLIT, share, rows), bf16),
        ((SPLIT, SPLIT - 1, share, rows), bf16),
        ((SPLIT - 1, share, rows), bf16),
        ((SPLIT - 1, share, rows), bf16),
    ]
    result = pl.pallas_call(
        functools.partial(mixer_kernel, rows * lax.axis_size("context")),
        out_shape=jax.ShapeDtypeStruct((SUBL, SPLIT, sub, rows), bf16),
        in_specs=[pl.BlockSpec(memory_space=pl.ANY)] * 7,
        out_specs=pl.BlockSpec(memory_space=pltpu.VMEM),
        scratch_shapes=[pltpu.VMEM(shape, kind) for shape, kind in scratch]
        + [pltpu.SemaphoreType.DMA((COPIES,))] * 2
        + [pltpu.SemaphoreType.DMA((7,))],
        compiler_params=pltpu.CompilerParams(
            collective_id=0, has_side_effects=True, vmem_limit_bytes=60 * 1024 * 1024
        ),
    )(
        q_proj, k_proj, v_proj, short_filter, residue, decay_rate,
        out_weight.reshape(SPLIT, sub, chans),
    )
    return result.reshape(SUBL * SPLIT * sub, rows)


def solution(mesh):
    return jax.shard_map(
        per_device,
        mesh=mesh,
        in_specs=(
            P("context", "tensor"),
            P("context", "tensor"),
            P("context", "tensor"),
            P(None, None, "tensor"),
            P(None, "tensor"),
            P(None, "tensor"),
            P("context", "tensor"),
        ),
        out_specs=P("tensor", "context"),
        check_vma=False,
    )
```

```python
import functools

import jax
import jax.numpy as jnp
from jax import lax
from jax.experimental import pallas as pl
from jax.experimental.pallas import tpu as pltpu
from jax.sharding import PartitionSpec as P

SPLIT = 4
RING = 16
LANES = 128
SUBL = 8
UP, DOWN = 7, 8
COPIES = 128


def mixer_kernel(
    total_rows, q_hbm, k_hbm, v_hbm, short_hbm, residue_hbm, rate_hbm, w_hbm, out_ref,
    q_ref, k_ref, v_ref, short_ref, residue_ref, rate_ref, w_ref, filt_ref, ext, head, p3, q3, g3, wide, rim_out, rim_in, st_out, st_in, whole, tokens,
    part, swapped, paired, crossed, summed, homed, send_sem, recv_sem, load_sem,
):
    rows = q_ref.shape[0]
    modes = rate_ref.shape[0]
    sub = w_ref.shape[1]
    place = lax.axis_index("context")
    blocks = lax.axis_size("context")
    y, z = place // RING, place % RING
    seat = lax.axis_index("tensor")
    x, core = seat // 2, seat % 2

    def on_context(distance):
        return {"context": lax.rem(place + (distance + blocks), blocks)}

    def on_ring(distance):
        return {"context": y * RING + lax.rem(z + (distance + RING), RING)}

    def on_x(distance):
        return {"tensor": lax.rem(seat + 2 * distance, 2 * SPLIT)}

    other_core = {"tensor": x * 2 + (1 - core)}
    peers = [on_context(1), on_context(-1)]
    peers += [on_context(d * RING) for d in range(1, SPLIT)]
    peers += [on_ring(1), on_ring(-1), other_core]
    peers += [on_x(d) for d in range(1, SPLIT)]
    barrier = pltpu.get_barrier_semaphore()
    for peer in peers:
        pl.semaphore_signal(barrier, inc=1, device_id=peer, device_id_type=pl.DeviceIdType.MESH)

    loads = []
    for src, dst in (
        (k_hbm, k_ref), (v_hbm, v_ref), (q_hbm, q_ref), (short_hbm, short_ref),
        (rate_hbm, rate_ref), (residue_hbm, residue_ref), (w_hbm, w_ref),
    ):
        loads.append(pltpu.make_async_copy(src, dst, load_sem.at[len(loads)]))
        loads[-1].start()

    started = []

    def send(src, dst, peer):
        index = len(started)
        copy = pltpu.make_async_remote_copy(
            src_ref=src,
            dst_ref=dst,
            send_sem=send_sem.at[index],
            recv_sem=recv_sem.at[index],
            device_id=peer,
            device_id_type=pl.DeviceIdType.MESH,
        )
        copy.start()
        started.append(copy)
        return copy

    taps, groups = short_ref.shape[1:]
    chans = q_ref.shape[1]
    owner = lax.broadcasted_iota(jnp.int32, (groups, chans), 1) // (chans // groups)
    own = owner == lax.broadcasted_iota(jnp.int32, (groups, chans), 0)
    spreader = jnp.where(own, 1.0, 0.0).astype(jnp.bfloat16)
    for load in loads:
        load.wait()
    for n in range(3):
        filt_ref[n, 0:taps, :] = lax.dot_general(
            short_ref[n], spreader, (((1,), (0,)), ((), ())), preferred_element_type=jnp.float32
        )
    rim_out[...] = jnp.zeros_like(rim_out)
    for n, src in enumerate((q_ref, k_ref, v_ref)):
        rim_out[2 * n : 2 * n + 2, :] = src[rows - 16 : rows, :].astype(jnp.float32)[14:16]

    def feature(which, src, lanes):
        ext[0:SUBL, :] = jnp.zeros((SUBL, LANES), jnp.float32)
        ext[SUBL : SUBL + rows, :] = src[:, lanes].astype(jnp.float32)
        total = filt_ref[which, 0:1, lanes] * ext[SUBL : SUBL + rows, :]
        for tap in range(1, 3):
            total = total + filt_ref[which, tap : tap + 1, lanes] * ext[
                SUBL - tap : SUBL - tap + rows, :
            ]
        return total.astype(jnp.bfloat16).astype(jnp.float32)

    for g in range(SUBL):
        lanes = slice(g * LANES, (g + 1) * LANES)
        spread = pl.ds(g, rows, stride=SUBL)
        k_feat = feature(1, k_ref, lanes)
        v_feat = feature(2, v_ref, lanes)
        p3[spread, :] = (k_feat * v_feat).astype(jnp.bfloat16).astype(jnp.float32)
        q3[spread, :] = feature(0, q_ref, lanes)
        wide[0, pl.ds(g, modes, stride=SUBL), :] = rate_ref[:, lanes] / total_rows
        wide[1, pl.ds(g, modes, stride=SUBL), :] = residue_ref[:, lanes]
    decay_step = wide[0]
    wide[2] = jnp.exp(-decay_step)
    wide[1] = wide[1] * jnp.sqrt(2.0 * decay_step)

    def mode_rows(slot):
        return [wide[slot, m * SUBL : (m + 1) * SUBL, :] for m in range(modes)]

    def run(first, last, state, gate):
        decay = mode_rows(2)
        scale = mode_rows(1) if gate else None
        unroll = 4

        def step(lap, state):
            for u in range(unroll):
                at = pl.ds(pl.multiple_of((lap * unroll + u) * SUBL, SUBL), SUBL)
                p = p3[at, :]
                state = tuple(a * s + p for a, s in zip(decay, state))
                if gate:
                    terms = [c * s for c, s in zip(scale, state)]
                    while len(terms) > 1:
                        terms = [terms[i] + terms[i + 1] for i in range(0, len(terms), 2)]
                    g3[at, :] = q3[at, :] * terms[0]
            return state

        return lax.fori_loop(first // unroll, last // unroll, step, state)

    zero = jnp.zeros((SUBL, LANES), jnp.float32)
    body_end = run(SUBL, rows, (zero,) * modes, False)
    whole[z, y] = w_ref[y]

    pl.semaphore_wait(barrier, len(peers))
    rim_copy = send(rim_out, rim_in, on_context(1))
    column = [None] + [
        send(w_ref.at[lax.rem(y + dy, SPLIT)], whole.at[z, y], on_context(dy * RING))
        for dy in range(1, SPLIT)
    ]

    def from_y(dy):
        return lax.rem(y + (SPLIT - dy), SPLIT)

    up = [[None] * SPLIT for _ in range(UP + 1)]
    down = [[None] * SPLIT for _ in range(DOWN + 1)]

    def ring(lap):
        for dy in range(SPLIT):
            source = from_y(dy)
            if lap == 0:
                if dy:
                    column[dy].wait_recv()
            for laps, count, sign in ((up, UP, 1), (down, DOWN, -1)):
                if lap > count:
                    continue
                if lap:
                    laps[lap][dy].wait_recv()
                if lap < count:
                    slot = whole.at[lax.rem(z + (RING - sign * lap), RING), source]
                    block = w_ref.at[y] if lap == 0 and dy == 0 else slot
                    laps[lap + 1][dy] = send(block, slot, on_ring(sign))

    rim_copy.wait_recv()
    rim = jnp.where(place > 0, rim_in[...], 0.0)
    feats = []
    for n, src in enumerate((q_ref, k_ref, v_ref)):
        head[0:SUBL, :] = jnp.zeros((SUBL, head.shape[1]), jnp.float32)
        head[SUBL - 2 : SUBL, :] = rim[2 * n : 2 * n + 2]
        head[SUBL : 2 * SUBL, :] = src[0:16, :].astype(jnp.float32)[0:SUBL]
        total = filt_ref[n, 0:1, :] * head[SUBL : 2 * SUBL, :]
        for tap in range(1, 3):
            total = total + filt_ref[n, tap : tap + 1, :] * head[
                SUBL - tap : 2 * SUBL - tap, :
            ]
        feats.append(total.astype(jnp.bfloat16).astype(jnp.float32))
    first_product = (feats[1] * feats[2]).astype(jnp.bfloat16).astype(jnp.float32)
    for g in range(SUBL):
        lanes = slice(g * LANES, (g + 1) * LANES)
        p3[pl.ds(g, SUBL, stride=SUBL), :] = first_product[:, lanes]
        q3[pl.ds(g, SUBL, stride=SUBL), :] = feats[0][:, lanes]
    head_end = jnp.concatenate(run(0, SUBL, (zero,) * modes, False), axis=0)
    state = jnp.concatenate(body_end, axis=0) + jnp.exp(-decay_step * (rows - SUBL)) * head_end

    half = RING // 2
    st_out[0] = state.astype(jnp.bfloat16)
    carried = {
        (1, 1): send(st_out.at[0], st_in.at[0], on_ring(1)),
        (-1, 1): send(st_out.at[0], st_in.at[half], on_ring(-1)),
    }
    before = jnp.zeros_like(state)
    after = state * jnp.exp(-decay_step * (rows * (RING - 1)))

    def turn(lap, before, after):
        for sign, count in ((1, half), (-1, half - 1)):
            if lap > count:
                continue
            slot = lap - 1 if sign > 0 else half + lap - 1
            carried[sign, lap].wait_recv()
            if lap < count:
                carried[sign, lap + 1] = send(st_in.at[slot], st_in.at[slot + 1], on_ring(sign))
        for sign, count in ((1, half), (-1, half - 1)):
            if lap > count:
                continue
            slot = lap - 1 if sign > 0 else half + lap - 1
            distance = lap if sign > 0 else RING - lap
            came = st_in[slot].astype(jnp.float32)
            if distance > 1:
                came = came * jnp.exp(-decay_step * (rows * (distance - 1)))
            earlier = z >= distance
            before = before + jnp.where(earlier, came, 0.0)
            after = after + jnp.where(earlier, 0.0, came)
        return before, after

    for lap in range(1, half + 1):
        before, after = turn(lap, before, after)
        if lap % 4:
            ring(lap - 1 - lap // 4)
    st_out[1] = (after + jnp.exp(-decay_step * (rows * RING)) * before).astype(jnp.bfloat16)
    rows_after = [
        send(st_out.at[1], st_in.at[RING - 2 + d], on_context(d * RING)) for d in range(1, SPLIT)
    ]
    ring(6)
    state = before
    for d in range(1, SPLIT):
        rows_after[d - 1].wait_recv()
        came = jnp.where(y >= d, st_in[RING - 2 + d].astype(jnp.float32), 0.0)
        if d > 1:
            came = came * jnp.exp(-decay_step * (rows * RING * (d - 1)))
        state = state + came

    run(0, rows, tuple(state[m * SUBL : (m + 1) * SUBL] for m in range(modes)), True)
    for g in range(SUBL):
        gated = g3[pl.ds(g, rows, stride=SUBL), :].astype(jnp.bfloat16)
        tokens[0, 0, :, g * LANES : (g + 1) * LANES] = gated[: rows // 2]
        tokens[0, 1, :, g * LANES : (g + 1) * LANES] = gated[rows // 2 :]

    from_below, from_above = on_context(RING), on_context(-RING)
    low = [send(tokens.at[0, h], tokens.at[1, h], from_below) for h in (0, 1)]
    high = [send(tokens.at[0, h], tokens.at[3, h], from_above) for h in (1, 0)]
    ring(7)
    low[0].wait_recv()
    across = [send(tokens.at[1, 0], tokens.at[2, 0], from_below)]
    high[0].wait_recv()
    across.append(send(tokens.at[3, 1], tokens.at[2, 1], from_above))
    ring(8)


    share = SUBL * sub

    def multiply(dy):
        rhs = tokens[dy].reshape(rows, -1)
        for half in range(2):
            lhs = whole[half * SUBL : (half + 1) * SUBL].reshape(SPLIT * share, -1)
            terms = lax.dot_general(
                lhs, rhs, (((1,), (1,)), ((), ())), preferred_element_type=jnp.float32
            ).astype(jnp.bfloat16)
            terms = terms.reshape(SUBL, SPLIT, sub, rows)
            for col in range(SPLIT):
                part[dy, half, col] = terms[:, col].reshape(share, rows)
        return send(part.at[dy, 1 - core], swapped.at[dy], other_core)

    def pair(dy, copy):
        copy.wait_recv()
        both = part[dy, core].astype(jnp.float32) + swapped[dy].astype(jnp.float32)
        paired[dy] = both.astype(jnp.bfloat16)
        return [
            send(paired.at[dy, lax.rem(x + dx, SPLIT)], crossed.at[dy, dx - 1], on_x(dx))
            for dx in range(1, SPLIT)
        ]

    def finish(dy, copies):
        total = paired[dy, x].astype(jnp.float32)
        for dx in range(1, SPLIT):
            copies[dx - 1].wait_recv()
            total = total + crossed[dy, dx - 1].astype(jnp.float32)
        total = total.astype(jnp.bfloat16)
        if dy == 0:
            out_ref[:, y] = total.reshape(SUBL, sub, rows)
            return None
        summed[dy - 1] = total
        return send(summed.at[dy - 1], homed.at[dy - 1], on_context(-dy * RING))

    swap0 = multiply(0)
    cross0 = pair(0, swap0)
    low[1].wait_recv()
    swap1 = multiply(1)
    cross1 = pair(1, swap1)
    high[1].wait_recv()
    swap3 = multiply(3)
    finish(0, cross0)
    cross3 = pair(3, swap3)
    for copy in across:
        copy.wait_recv()
    swap2 = multiply(2)
    home1 = finish(1, cross1)
    cross2 = pair(2, swap2)
    home3 = finish(3, cross3)
    home2 = finish(2, cross2)
    for dy, copy in ((1, home1), (3, home3), (2, home2)):
        copy.wait_recv()
        out_ref[:, lax.rem(y + dy, SPLIT)] = homed[dy - 1].reshape(SUBL, sub, rows)
    for copy in started:
        copy.wait_send()


def per_device(q_proj, k_proj, v_proj, short_filter, residue, decay_rate, out_weight):
    rows, chans = q_proj.shape
    modes = residue.shape[0]
    sub = out_weight.shape[0] // SPLIT
    share = SUBL * sub
    f32, bf16 = jnp.float32, jnp.bfloat16
    scratch = [
        ((rows, chans), bf16),
        ((rows, chans), bf16),
        ((rows, chans), bf16),
        (short_filter.shape, bf16),
        (residue.shape, f32),
        (decay_rate.shape, f32),
        ((SPLIT, sub, chans), bf16),
        ((3, SUBL, chans), f32),
        ((rows + SUBL, LANES), f32),
        ((2 * SUBL, chans), f32),
        ((rows * SUBL, LANES), f32),
        ((rows * SUBL, LANES), f32),
        ((rows * SUBL, LANES), f32),
        ((3, modes * SUBL, LANES), f32),
        ((SUBL, chans), f32),
        ((SUBL, chans), f32),
        ((2, modes * SUBL, LANES), bf16),
        ((RING + 2, modes * SUBL, LANES), bf16),
        ((RING, SPLIT, sub, chans), bf16),
        ((SPLIT, 2, rows // 2, chans), bf16),
        ((SPLIT, 2, SPLIT, share, rows), bf16),
        ((SPLIT, SPLIT, share, rows), bf16),
        ((SPLIT, SPLIT, share, rows), bf16),
        ((SPLIT, SPLIT - 1, share, rows), bf16),
        ((SPLIT - 1, share, rows), bf16),
        ((SPLIT - 1, share, rows), bf16),
    ]
    result = pl.pallas_call(
        functools.partial(mixer_kernel, rows * lax.axis_size("context")),
        out_shape=jax.ShapeDtypeStruct((SUBL, SPLIT, sub, rows), bf16),
        in_specs=[pl.BlockSpec(memory_space=pl.ANY)] * 7,
        out_specs=pl.BlockSpec(memory_space=pltpu.VMEM),
        scratch_shapes=[pltpu.VMEM(shape, kind) for shape, kind in scratch]
        + [pltpu.SemaphoreType.DMA((COPIES,))] * 2
        + [pltpu.SemaphoreType.DMA((7,))],
        compiler_params=pltpu.CompilerParams(
            collective_id=0, has_side_effects=True, vmem_limit_bytes=60 * 1024 * 1024
        ),
    )(
        q_proj, k_proj, v_proj, short_filter, residue, decay_rate,
        out_weight.reshape(SPLIT, sub, chans),
    )
    return result.reshape(SUBL * SPLIT * sub, rows)


def solution(mesh):
    return jax.shard_map(
        per_device,
        mesh=mesh,
        in_specs=(
            P("context", "tensor"),
            P("context", "tensor"),
            P("context", "tensor"),
            P(None, None, "tensor"),
            P(None, "tensor"),
            P(None, "tensor"),
            P("context", "tensor"),
        ),
        out_specs=P("tensor", "context"),
        check_vma=False,
    )
```
